32 devices in a mesh: sub: 4 (over y, x), tile: 8 (over z, core).
Axes of the slice: x: 2, y: 2, z: 4, core: 2. Of those that a mesh axis runs over, the one named last changes fastest.
Arguments:
- echoes: bfloat16 [2, 2048, 16384], P(None, 'sub', 'tile'), may hold values from -6 to 6
- steering: bfloat16 [2, 2048, 64], P(None, ('sub', 'tile')), may hold values from -0.5 to 0.5
- interp: bfloat16 [81920], replicated, may hold values from -6 to 6
- angles: float32 [8, 4, 2, 2, 16384], P('tile', 'sub'), may hold values from -3.140625 to 3.140625
- range_map: bfloat16 [8, 16384, 1024], P('tile', 'sub'), may hold values from -0.0234375 to 0.0234375
- beam_map: bfloat16 [8, 8, 256, 256], P('tile'), may hold values from -0.375 to 0.375
- footprint: int32 [8, 4], P('tile'), may hold values from 0 to 7, all different within a row
Outputs:
- image_tile: float32 [2, 2048, 1024], P(None, 'tile', 'sub')
The draws below stay inside these ranges and needn't reach their ends.
Inputs may be any that keep to these rules, and one draw needn't show every extreme that they name: `footprint`: each row names 4 different tiles, and every tile is named by some row.
All inputs are finite; a program needn't handle non-finite values.
Results may differ from the reference program's by a relative error of at most 0.018.
Values may be sent and summed in bfloat16 or wider, within the bound.
No kernel may reach another device: no remote copies, remote signals or barrier semaphores. Data moves between devices by JAX's collectives and lax.ppermute only.
A program may use at most 128 MiB of HBM per device.

```python
import jax
import jax.numpy as jnp
from jax import lax

GATES = 16384
P_DEV = 64
TR = 256
TC = 1024
FOOT = 4
LV = 2
PULSES = 2048
BF = 256
INTERP_LEN = 81920
N_SUB = 4
N_TILE = 8


def block_levels(key, shape, cuts, least, top_value):
    def one(position, shards_of):
        heights = jax.random.uniform(jax.random.fold_in(jax.random.fold_in(key, 6), position), (shards_of,), jnp.float32, least / len(cuts), top_value / len(cuts))
        return jnp.repeat(jnp.exp(heights), shape[position] // shards_of).reshape((-1,) + (1,) * (len(shape) - position - 1))

    gain = one(*cuts[0])
    for cut in cuts[1:]:
        gain = gain * one(*cut)
    return gain


def different_ones(stream_key, rows, amount, top, lift):
    order = jax.random.permutation(jax.random.fold_in(stream_key, 1), amount)
    favour = order
    for power in range(3):
        favour = favour * favour // amount
    favour = favour * lift // amount
    chance = jax.random.randint(jax.random.fold_in(stream_key, 2), (rows, amount), 0, 4096) + favour
    sure = jax.random.permutation(jax.random.fold_in(stream_key, 3), rows)[jnp.arange(amount) % rows]
    chance = jnp.where(jnp.arange(rows)[:, None] == sure[None, :], 1 << 14, chance)
    priority = chance * amount + jnp.arange(amount)
    return lax.top_k(priority.astype(jnp.int32), top)[1].astype(jnp.int32)


def normal_values(rng, extent, deviation, reach, cuts=(), kind=jnp.bfloat16):
    values = jax.random.normal(rng, extent, jnp.float32) * deviation
    if len(cuts) > 0:
        values = block_levels(rng, extent, cuts, -0.22, 0.18) * values
    return jnp.clip(values, min=-reach, max=reach).astype(kind)


def setup_inputs(seed: int = 0) -> dict:
    seeds = jax.random.split(jax.random.key(seed), 8)
    echoes = normal_values(seeds[0], (2, PULSES, GATES), 1.0, 6.0, ((1, 4), (2, 8)))
    steering = normal_values(seeds[1], (2, PULSES, P_DEV), (2 * P_DEV) ** -0.5, 0.5, ((1, 32),))
    interp = normal_values(seeds[2], (INTERP_LEN,), 1.0, 6.0)
    angles = jnp.clip(jax.random.uniform(seeds[3], (N_TILE, N_SUB, LV, 2, GATES), jnp.float32, -3.140625, 3.140625), -3.140625, 3.140625)
    range_map = normal_values(seeds[4], (N_TILE, GATES, TC), (GATES * FOOT) ** -0.5, 0.0234375, ((0, 8), (1, 4)))
    beam_map = normal_values(seeds[5], (N_TILE, N_TILE, TR, BF), BF ** -0.5, 0.375, ((0, 8),))
    footprint = different_ones(seeds[6], N_TILE, N_TILE, FOOT, 8192)
    return dict(echoes=echoes, steering=steering, interp=interp, angles=angles, range_map=range_map, beam_map=beam_map, footprint=footprint)


def rotate(values, phase_sum):
    cosine = jnp.cos(phase_sum)
    sine_val = jnp.sin(phase_sum)
    return jnp.stack([cosine * values[0] - sine_val * values[1], sine_val * values[0] + cosine * values[1]])


def reference(echoes, steering, interp, angles, range_map, beam_map, footprint):
    levels = N_SUB.bit_length() - 1
    blocks = echoes.reshape(2, N_SUB, N_TILE, P_DEV, GATES)
    steer_blocks = steering.reshape(2, N_SUB, N_TILE, P_DEV, P_DEV)
    maps_all = range_map.reshape(N_TILE, N_SUB, GATES // N_SUB, TC)
    tile_ids = jnp.arange(N_TILE, dtype=jnp.int32)
    sub_ids = jnp.arange(N_SUB, dtype=jnp.int32)

    def column(carry, tile_idx):
        pulses = lax.dynamic_index_in_dim(blocks, tile_idx, 2, False)
        steer = lax.dynamic_index_in_dim(steer_blocks, tile_idx, 2, False)
        products = jnp.einsum("csbp,dspg->cdsbg", steer.astype(jnp.float32), pulses.astype(jnp.float32))
        polar_image = jnp.stack([products[0, 0] - products[1, 1], products[0, 1] + products[1, 0]]).astype(jnp.bfloat16)
        ang_tile = lax.dynamic_index_in_dim(angles, tile_idx, 0, False)
        offset = 0
        for merge_level in range(levels):
            beam_count = polar_image.shape[2]
            half_len = polar_image.shape[3] // 2
            upper_side = (sub_ids >> merge_level) & 1
            partner = polar_image[:, sub_ids ^ (1 << merge_level)]
            is_upper = (upper_side == 1)[None, :, None, None]
            lower_full = jnp.where(is_upper, partner, polar_image)
            upper_full = jnp.where(is_upper, polar_image, partner)
            lower_half = jnp.where(is_upper, lower_full[..., half_len:], lower_full[..., :half_len])
            upper_half = jnp.where(is_upper, upper_full[..., half_len:], upper_full[..., :half_len])
            weight_len = 4 * beam_count * beam_count
            weights = interp[offset:offset + weight_len].reshape(2, 2 * beam_count, beam_count)
            offset = offset + weight_len
            merged = jnp.zeros((2, N_SUB, 2 * beam_count, half_len), jnp.float32)
            for child_idx, source in ((0, lower_half), (1, upper_half)):
                mapped = jnp.einsum("ob,csbr->csor", weights[child_idx].astype(jnp.float32), source.astype(jnp.float32))
                beam_angle = ang_tile[:, merge_level, child_idx, :2 * beam_count]
                range_angle = ang_tile[:, merge_level, child_idx, 2 * beam_count:2 * beam_count + half_len]
                phase_sum = beam_angle[:, :, None] + range_angle[:, None, :]
                merged = merged + rotate(mapped, phase_sum)
            norm_scale = (2.0 * beam_count) ** -0.5
            polar_image = (norm_scale * merged).astype(jnp.bfloat16)
        range_tile = lax.dynamic_index_in_dim(maps_all, tile_idx, 0, False)
        query_rows = jnp.einsum("csbr,srx->csbx", polar_image.astype(jnp.float32), range_tile.astype(jnp.float32)).astype(jnp.bfloat16)
        beam_tile = lax.dynamic_index_in_dim(beam_map, tile_idx, 0, False)
        foot_row = lax.dynamic_index_in_dim(footprint, tile_idx, 0, False)
        chosen = beam_tile[foot_row]
        picked_terms = jnp.einsum("fib,csbx->cfix", chosen.astype(jnp.float32), query_rows.astype(jnp.float32))
        onehot = (foot_row[None, :] == tile_ids[:, None]).astype(jnp.float32)
        placed = jnp.einsum("kf,cfix->ckix", onehot, picked_terms, precision=lax.Precision.HIGHEST)
        return carry + placed, None

    start = jnp.zeros((2, N_TILE, TR, TC), jnp.float32)
    total, _ = lax.scan(column, start, tile_ids)
    return total.reshape(2, N_TILE * TR, TC)
```

```python
import functools

import jax
import jax.numpy as jnp
from jax import lax
from jax.experimental import pallas as pl
from jax.experimental.pallas import tpu as pltpu
from jax.sharding import PartitionSpec as P


PARTS = 8
CHUNKS = (2, 2, 2, 2)


def swap(block, axis, mask):
    count = lax.axis_size(axis)
    return lax.ppermute(block, axis, [(i, i ^ mask) for i in range(count)])


def cost(flops, nbytes):
    return pl.CostEstimate(flops=int(flops), bytes_accessed=int(nbytes), transcendentals=0)


def mirrored(value, bits):
    result = value * 0
    for low in range(bits):
        result = result | (((value >> low) & 1) << (bits - 1 - low))
    return result


def cut_kernel(count, ids_ref, *refs):
    for k in range(count):
        refs[count + k][...] = refs[k][...]


def cut_blocks(echoes, ids, first, length, unit, rows):
    count = lax.axis_size("tile")
    planes = echoes.shape[0]

    def pick(k):
        return pl.BlockSpec((planes, rows, unit), lambda i, ids_ref: (0, ids_ref[k], first + i))

    shape = (planes, rows, length * unit)
    return pl.pallas_call(
        functools.partial(cut_kernel, count - 1),
        out_shape=[jax.ShapeDtypeStruct(shape, echoes.dtype)] * (count - 1),
        grid_spec=pltpu.PrefetchScalarGridSpec(
            num_scalar_prefetch=1,
            grid=(length,),
            in_specs=[pick(k) for k in range(1, count)],
            out_specs=[pl.BlockSpec((planes, rows, unit), lambda i, ids_ref: (0, 0, i))] * (count - 1),
        ),
        cost_estimate=cost(0, 2 * (count - 1) * planes * rows * length * unit * 2),
        name="cut_blocks",
    )(ids, *[echoes] * (count - 1))


def steer_kernel(count, subs, ids_ref, weights_ref, *refs):
    sources, outs, held = refs[:count], refs[count:-1], refs[-1]
    weights = weights_ref[...]
    for k in range(count):
        block = sources[k][...]
        block = block.reshape(block.shape[0] * block.shape[1], block.shape[2])
        beams = jnp.dot(weights, block, preferred_element_type=jnp.float32)
        held[ids_ref[count + k], ids_ref[2 * count + k]] = beams.astype(held.dtype)
    for r in range(subs):
        outs[r][...] = held[r]


def steer_blocks(echoes, arrived, weights, ids, first, length, unit, rows):
    count, subs = lax.axis_size("tile"), lax.axis_size("sub")
    pieces = count // subs
    planes = echoes.shape[0]
    height = weights.shape[0]
    block = (planes, rows, unit)
    return pl.pallas_call(
        functools.partial(steer_kernel, count, subs),
        out_shape=[jax.ShapeDtypeStruct((pieces, height, length * unit), echoes.dtype)] * subs,
        grid_spec=pltpu.PrefetchScalarGridSpec(
            num_scalar_prefetch=1,
            grid=(length,),
            in_specs=[pl.BlockSpec(weights.shape, lambda i, ids_ref: (0, 0))]
            + [pl.BlockSpec(block, lambda i, ids_ref: (0, ids_ref[0], first + i))]
            + [pl.BlockSpec(block, lambda i, ids_ref: (0, 0, i))] * (count - 1),
            out_specs=[pl.BlockSpec((pieces, height, unit), lambda i, ids_ref: (0, 0, i))] * subs,
            scratch_shapes=[pltpu.VMEM((subs, pieces, height, unit), echoes.dtype)],
        ),
        cost_estimate=cost(
            2 * count * height * height * length * unit, 4 * count * height * length * unit
        ),
        name="steer_blocks",
    )(ids, weights, echoes, *arrived)


def turned(block, cosine, sine):
    half = block.shape[0] // 2
    real = block[:half].astype(jnp.float32)
    imag = block[half:].astype(jnp.float32)
    return [
        (real * cosine - imag * sine).astype(jnp.bfloat16),
        (real * sine + imag * cosine).astype(jnp.bfloat16),
    ]


def merge_kernel(levels, subs, given, final, steps, ids_ref, *refs):
    sources = [ref[0] for ref in refs[:subs]]
    phases_ref = refs[subs]
    mats = refs[subs + 1 : subs + 1 + levels]
    map_ref = refs[subs + 1 + levels]
    rest = refs[subs + 2 + levels :]
    if given:
        before, rest = rest[0], rest[1:]
    total = rest[-1] if final else rest[0]
    step = pl.program_id(0) * pl.num_programs(1) + pl.program_id(1)

    @pl.when(step == 0)
    def _():
        total[...] = before[...] if given else jnp.zeros_like(total)

    row = 0
    for level in range(levels):
        merged = []
        for h in range(len(sources) // 2):
            stacked = []
            for child in range(2):
                cosine = phases_ref[0, row : row + 1, :]
                sine = phases_ref[0, row + 1 : row + 2, :]
                row += 2
                stacked += turned(sources[2 * h + child], cosine, sine)
            product = jnp.dot(
                mats[level][h], jnp.concatenate(stacked, axis=0), preferred_element_type=jnp.float32
            )
            merged.append(product.astype(jnp.bfloat16))
        sources = merged
    total[...] += jnp.dot(sources[0], map_ref[0], preferred_element_type=jnp.float32)
    if final:
        width = total.shape[1] // subs

        @pl.when(step == steps - 1)
        def _():
            for r in range(subs):
                start = pl.multiple_of(ids_ref[r] * width, width)
                rest[r][...] = total[:, pl.ds(start, width)].astype(rest[r].dtype)


def merge_blocks(sources, phases, mats, range_map, ids, before, final, first, length, unit):
    subs, levels = len(sources), len(mats)
    pieces, height = sources[0].shape[:2]
    columns = range_map.shape[2]
    beams = mats[-1].shape[1]
    steps = length * pieces
    given = before is not None

    def whole(array):
        return pl.BlockSpec(array.shape, lambda i, e, ids_ref: (0,) * array.ndim)

    in_specs = [pl.BlockSpec((1, height, unit), lambda i, e, ids_ref: (e, 0, i))] * subs
    in_specs += [pl.BlockSpec((1, phases.shape[1], unit), lambda i, e, ids_ref: (e, 0, first + i))]
    in_specs += [whole(mat) for mat in mats]
    in_specs += [pl.BlockSpec((1, unit, columns), lambda i, e, ids_ref: (e, first + i, 0))]
    operands = [ids, *sources, phases, *mats, range_map]
    scratch, aliases = [], {}
    if given:
        in_specs.append(pl.BlockSpec((beams, columns), lambda i, e, ids_ref: (0, 0)))
        operands.append(before)
    if final:
        width = columns // subs
        out_shape = [jax.ShapeDtypeStruct((beams, width), jnp.bfloat16)] * subs
        out_specs = [pl.BlockSpec((beams, width), lambda i, e, ids_ref: (0, 0))] * subs
        scratch = [pltpu.VMEM((beams, columns), jnp.float32)]
    else:
        out_shape = jax.ShapeDtypeStruct((beams, columns), jnp.float32)
        out_specs = pl.BlockSpec((beams, columns), lambda i, e, ids_ref: (0, 0))
        if given:
            aliases = {len(operands) - 1: 0}
    flops = sum(2 * mat.size for mat in mats) * steps * unit + 2 * beams * columns * steps * unit
    moved = 2 * range_map.shape[2] * steps * unit + 2 * subs * height * steps * unit
    return pl.pallas_call(
        functools.partial(merge_kernel, levels, subs, given, final, steps),
        out_shape=out_shape,
        grid_spec=pltpu.PrefetchScalarGridSpec(
            num_scalar_prefetch=1,
            grid=(length, pieces),
            in_specs=in_specs,
            out_specs=out_specs,
            scratch_shapes=scratch,
        ),
        input_output_aliases=aliases,
        cost_estimate=cost(flops, moved),
        name="merge_blocks",
    )(*operands)


def beam_kernel(subs, ids_ref, *refs):
    pieces = refs[:subs]
    near_ref, far_ref, keep_ref, send_ref, held = refs[subs:]
    step = pl.program_id(0)
    count = pl.num_programs(0)

    @pl.when(step == 0)
    def _():
        total = pieces[0][...].astype(jnp.float32)
        for piece in pieces[1:]:
            total = total + piece[...].astype(jnp.float32)
        held[...] = total.astype(held.dtype)

    planes = keep_ref.shape[1]
    depth = held.shape[0] // planes
    for side, map_ref, out_ref in ((0, near_ref, keep_ref), (1, far_ref, send_ref)):
        covered = ids_ref[2 * count + 2 * step + side] == 1

        @pl.when(covered)
        def _():
            for plane in range(planes):
                out_ref[0, plane] = jnp.dot(
                    map_ref[0],
                    held[plane * depth : (plane + 1) * depth],
                    preferred_element_type=jnp.float32,
                ).astype(out_ref.dtype)

        @pl.when(jnp.logical_not(covered))
        def _():
            out_ref[...] = jnp.zeros_like(out_ref)


def beam_blocks(pieces, beam_map, ids):
    tiles, rows, depth = beam_map.shape
    count = tiles // 2
    height, width = pieces[0].shape
    planes = height // depth
    shape = (count, planes, rows, width)

    def pick(side):
        return pl.BlockSpec((1, rows, depth), lambda i, ids_ref: (ids_ref[2 * i + side], 0, 0))

    out_spec = pl.BlockSpec((1, planes, rows, width), lambda i, ids_ref: (i, 0, 0, 0))
    return pl.pallas_call(
        functools.partial(beam_kernel, len(pieces)),
        out_shape=[
            jax.ShapeDtypeStruct(shape, jnp.float32),
            jax.ShapeDtypeStruct(shape, jnp.bfloat16),
        ],
        grid_spec=pltpu.PrefetchScalarGridSpec(
            num_scalar_prefetch=1,
            grid=(count,),
            in_specs=[pl.BlockSpec((height, width), lambda i, ids_ref: (0, 0))] * len(pieces)
            + [pick(0), pick(1)],
            out_specs=[out_spec, out_spec],
            scratch_shapes=[pltpu.VMEM((height, width), jnp.bfloat16)],
        ),
        cost_estimate=cost(2 * tiles * rows * depth * planes * width, 2 * beam_map.size),
        name="beam_blocks",
    )(ids, *pieces, beam_map, beam_map)


def merge_tables(interp, angles, gates, base, piece, pieces):
    sub_index, subs = lax.axis_index("sub"), lax.axis_size("sub")
    levels = subs.bit_length() - 1
    mats, rows, offset = [], [], 0
    for level in range(levels):
        beams = base << level
        upper = (sub_index >> level) & 1
        higher = sub_index >> (level + 1)
        size = 4 * beams * beams
        weights = interp[offset : offset + size].reshape(2, 2 * beams, beams).astype(jnp.float32)
        offset += size
        weights = jnp.where(upper == 1, weights[::-1], weights) * (2.0 * beams) ** -0.5
        group = []
        for h in range(subs >> (level + 1)):
            start = 2 * beams
            for bit in range(levels - level - 1):
                start = start + (((higher ^ h) >> bit) & 1) * (gates >> (level + 2 + bit))
            packet = jnp.concatenate(
                [
                    angles[level, :, : 2 * beams],
                    lax.dynamic_slice_in_dim(angles[level], start, piece, 1),
                ],
                axis=1,
            )
            if h:
                packet = swap(packet, "sub", h << (level + 1))
            packet = jnp.where(upper == 1, packet[::-1], packet)
            cosine, sine = jnp.cos(packet), jnp.sin(packet)
            real = cosine[:, : 2 * beams, None] * weights
            imag = sine[:, : 2 * beams, None] * weights
            group.append(
                jnp.concatenate(
                    [
                        jnp.concatenate([real[0], -imag[0], real[1], -imag[1]], axis=1),
                        jnp.concatenate([imag[0], real[0], imag[1], real[1]], axis=1),
                    ],
                    axis=0,
                ).astype(jnp.bfloat16)
            )
            for child in range(2):
                rows += [cosine[child, 2 * beams :], sine[child, 2 * beams :]]
        mats.append(jnp.stack(group))
    rows += [jnp.zeros_like(rows[0])] * (-len(rows) % 8)
    phases = jnp.stack(rows).reshape(len(rows), pieces, piece // pieces)
    return mats, phases.transpose(1, 0, 2)


def on_device(echoes, steering, interp, angles, range_map, beam_map, footprint):
    tiles, subs = lax.axis_size("tile"), lax.axis_size("sub")
    tile_index, sub_index = lax.axis_index("tile"), lax.axis_index("sub")
    pieces = tiles // subs
    local = echoes.shape[2]
    base = steering.shape[1]
    unit = local // PARTS
    bits = subs.bit_length() - 1

    sources = [tile_index ^ k for k in range(tiles)]
    slots = [sub_index ^ mirrored(source // pieces, bits) for source in sources]
    spots = [source % pieces for source in sources]
    ids = jnp.stack(sources + slots + spots).astype(jnp.int32)
    column_ids = jnp.stack([sub_index ^ r for r in range(subs)]).astype(jnp.int32)

    stretches, first = [], 0
    for length in CHUNKS:
        stretches.append((first, length))
        first += length

    arrived = []
    for first, length in stretches:
        cuts = cut_blocks(echoes, ids, first, length, unit, base)
        order = sorted(range(1, tiles), reverse=True)
        got = {k: swap(cuts[k - 1], "tile", k) for k in order}
        arrived.append([got[k] for k in range(1, tiles)])

    steer = jnp.concatenate(
        [
            jnp.concatenate([steering[0], -steering[1]], axis=1),
            jnp.concatenate([steering[1], steering[0]], axis=1),
        ],
        axis=0,
    )
    mats, phases = merge_tables(interp, angles[0, 0], local * tiles, base, local * pieces, pieces)
    map_rows = range_map[0].reshape(pieces, local, range_map.shape[2])

    total = None
    for (first, length), blocks in zip(stretches, arrived):
        parts = steer_blocks(echoes, blocks, steer, ids, first, length, unit, base)
        parts = [parts[0]] + [swap(parts[r], "sub", r) for r in range(1, subs)]
        final = first + length == PARTS
        total = merge_blocks(
            parts, phases, mats, map_rows, column_ids, total, final, first, length, unit
        )

    quarters = [total[0]] + [swap(total[r], "sub", r) for r in range(1, subs)]
    tile_ids = jnp.arange(tiles, dtype=jnp.int32)
    covered = jnp.any(footprint[0][None, :] == tile_ids[:, None], axis=1).astype(jnp.int32)
    order = tile_index ^ tile_ids
    beam_ids = jnp.concatenate([order, covered[order]]).astype(jnp.int32)
    keep, send = beam_blocks(quarters, beam_map[0], beam_ids)
    other = swap(send, "tile", 1)
    image = keep[0] + other[0].astype(jnp.float32)
    sums = [
        (keep[d] + other[d].astype(jnp.float32)).astype(jnp.bfloat16) for d in range(1, tiles // 2)
    ]
    for d in range(1, tiles // 2):
        image = image + swap(sums[d - 1], "tile", 2 * d).astype(jnp.float32)
    return image


def solution(mesh):
    placed = (
        P(None, "sub", "tile"),
        P(None, ("sub", "tile"), None),
        P(),
        P("tile", "sub", None, None, None),
        P("tile", "sub", None),
        P("tile", None, None, None),
        P("tile", None),
    )
    return jax.shard_map(
        on_device, mesh=mesh, in_specs=placed, out_specs=P(None, "tile", "sub"), check_vma=False
    )
```

```python
import functools

import jax
import jax.numpy as jnp
from jax import lax
from jax.experimental import pallas as pl
from jax.experimental.pallas import tpu as pltpu
from jax.sharding import PartitionSpec as P


PARTS = 8
CHUNKS = (3, 2, 2, 1)
GRANT = 24 << 20


def swap(block, axis, mask):
    count = lax.axis_size(axis)
    return lax.ppermute(block, axis, [(i, i ^ mask) for i in range(count)])


def cost(flops, nbytes):
    return pl.CostEstimate(flops=int(flops), bytes_accessed=int(nbytes), transcendentals=0)


def mirrored(value, bits):
    result = value * 0
    for low in range(bits):
        result = result | (((value >> low) & 1) << (bits - 1 - low))
    return result


def masks(count):
    return list(range(count - 1, 0, -1))


def lanes(start):
    return pl.multiple_of(start, 128)


def window(shape, offsets):
    return pl.BlockSpec(tuple(pl.Element(size) for size in shape), offsets)


def params():
    return pltpu.CompilerParams(vmem_limit_bytes=GRANT)


def cut_kernel(count, ids_ref, *refs):
    for k in range(count):
        refs[count + k][...] = refs[k][...]


def cut_blocks(echoes, ids, first, length, unit, rows):
    count = lax.axis_size("tile")
    planes = echoes.shape[0]

    def pick(k):
        return window(
            (planes, rows, unit), lambda i, ids_ref: (0, pl.multiple_of(ids_ref[k] * rows, rows), lanes(first + i * unit))
        )

    shape = (planes, rows, length * unit)
    return pl.pallas_call(
        functools.partial(cut_kernel, count - 1),
        out_shape=[jax.ShapeDtypeStruct(shape, echoes.dtype)] * (count - 1),
        grid_spec=pltpu.PrefetchScalarGridSpec(
            num_scalar_prefetch=1,
            grid=(length,),
            in_specs=[pick(k) for k in masks(count)],
            out_specs=[pl.BlockSpec((planes, rows, unit), lambda i, ids_ref: (0, 0, i))] * (count - 1),
        ),
        compiler_params=params(),
        cost_estimate=cost(0, 2 * (count - 1) * planes * rows * length * unit * 2),
        name="cut_blocks",
    )(ids, *[echoes] * (count - 1))


def lend_kernel(count, ids_ref, *refs):
    for d in range(count):
        refs[count][d] = refs[d][...]


def lend_blocks(echoes, ids, first, length, unit, rows):
    count = lax.axis_size("tile") // 2
    planes = echoes.shape[0]

    def pick(d):
        return window(
            (planes, rows, unit),
            lambda i, ids_ref: (0, pl.multiple_of(ids_ref[2 * d + 1] * rows, rows), lanes(first + i * unit)),
        )

    return pl.pallas_call(
        functools.partial(lend_kernel, count),
        out_shape=jax.ShapeDtypeStruct((count, planes, rows, length * unit), echoes.dtype),
        grid_spec=pltpu.PrefetchScalarGridSpec(
            num_scalar_prefetch=1,
            grid=(length,),
            in_specs=[pick(d) for d in range(count)],
            out_specs=pl.BlockSpec((count, planes, rows, unit), lambda i, ids_ref: (0, 0, 0, i)),
        ),
        compiler_params=params(),
        cost_estimate=cost(0, 4 * count * planes * rows * length * unit),
        name="lend_blocks",
    )(ids, *[echoes] * count)


def join_kernel(count, ids_ref, *refs):
    for d in range(count):
        refs[2 * count + d][0] = refs[2 * d][...]
        refs[2 * count + d][1] = refs[2 * d + 1][0]


def join_blocks(echoes, lent, ids, first, behind, length, unit, rows):
    count = lax.axis_size("tile") // 2
    planes = echoes.shape[0]
    in_specs, operands = [], []
    for d in masks(count):
        in_specs += [
            window(
                (planes, rows, unit),
                lambda i, ids_ref, d=d: (0, pl.multiple_of(ids_ref[2 * d] * rows, rows), lanes(first + i * unit)),
            ),
            window(
                (1, planes, rows, unit),
                lambda i, ids_ref, d=d: (d, 0, 0, lanes(first - behind + i * unit)),
            ),
        ]
        operands += [echoes, lent]
    shape = (2, planes, rows, length * unit)
    return pl.pallas_call(
        functools.partial(join_kernel, count - 1),
        out_shape=[jax.ShapeDtypeStruct(shape, echoes.dtype)] * (count - 1),
        grid_spec=pltpu.PrefetchScalarGridSpec(
            num_scalar_prefetch=1,
            grid=(length,),
            in_specs=in_specs,
            out_specs=[pl.BlockSpec((2, planes, rows, unit), lambda i, ids_ref: (0, 0, 0, i))]
            * (count - 1),
        ),
        compiler_params=params(),
        cost_estimate=cost(0, 8 * (count - 1) * planes * rows * length * unit),
        name="join_blocks",
    )(ids, *operands)


def steer_kernel(count, subs, paired, ids_ref, weights_ref, *refs):
    outs, held = refs[-1 - subs : -1], refs[-1]
    weights = weights_ref[...]
    for k in range(count):
        if paired and k:
            block = refs[1][0] if k == 1 else refs[1 + count // 2 - k // 2][k % 2]
        else:
            block = refs[count - k if k else 0][...]
        block = block.reshape(block.shape[0] * block.shape[1], block.shape[2])
        beams = jnp.dot(weights, block, preferred_element_type=jnp.float32)
        held[ids_ref[count + k], ids_ref[2 * count + k]] = beams.astype(held.dtype)
    for r in range(subs):
        outs[r][...] = held[r]


def steer_blocks(echoes, lent, arrived, weights, ids, first, behind, length, unit, rows, after):
    count, subs = lax.axis_size("tile"), lax.axis_size("sub")
    pieces = count // subs
    planes = echoes.shape[0]
    height = weights.shape[0]
    block = (planes, rows, unit)
    paired = lent is not None
    in_specs = [
        pl.BlockSpec(weights.shape, lambda i, ids_ref: (0, 0)),
        window(block, lambda i, ids_ref: (0, pl.multiple_of(ids_ref[0] * rows, rows), lanes(first + i * unit))),
    ]
    operands = [ids, weights, echoes]
    if paired:
        in_specs.append(
            window((1,) + block, lambda i, ids_ref: (0, 0, 0, lanes(first - behind + i * unit)))
        )
        operands.append(lent)
        in_specs += [pl.BlockSpec((2,) + block, lambda i, ids_ref: (0, 0, 0, i))] * len(arrived)
    else:
        in_specs += [pl.BlockSpec(block, lambda i, ids_ref: (0, 0, i))] * len(arrived)
    operands += arrived
    in_specs += [pl.BlockSpec(memory_space=pl.ANY)] * len(after)
    operands += after
    return pl.pallas_call(
        functools.partial(steer_kernel, count, subs, paired),
        out_shape=[jax.ShapeDtypeStruct((pieces, height, length * unit), echoes.dtype)] * subs,
        grid_spec=pltpu.PrefetchScalarGridSpec(
            num_scalar_prefetch=1,
            grid=(length,),
            in_specs=in_specs,
            out_specs=[pl.BlockSpec((pieces, height, unit), lambda i, ids_ref: (0, 0, i))] * subs,
            scratch_shapes=[pltpu.VMEM((subs, pieces, height, unit), echoes.dtype)],
        ),
        compiler_params=params(),
        cost_estimate=cost(
            2 * count * height * height * length * unit, 4 * count * height * length * unit
        ),
        name="steer_blocks",
    )(*operands)


def turned(block, cosine, sine):
    half = block.shape[0] // 2
    real = block[:half].astype(jnp.float32)
    imag = block[half:].astype(jnp.float32)
    return [
        (real * cosine - imag * sine).astype(jnp.bfloat16),
        (real * sine + imag * cosine).astype(jnp.bfloat16),
    ]


def merge_kernel(levels, subs, given, final, steps, ids_ref, *refs):
    sources = [ref[0] for ref in refs[:subs]]
    phases_ref = refs[subs]
    mats = refs[subs + 1 : subs + 1 + levels]
    map_ref = refs[subs + 1 + levels]
    rest = refs[subs + 2 + levels :]
    if given:
        before, rest = rest[0], rest[1:]
    total = rest[-1] if final else rest[0]
    step = pl.program_id(0) * pl.num_programs(1) + pl.program_id(1)

    @pl.when(step == 0)
    def _():
        total[...] = before[...] if given else jnp.zeros_like(total)

    row = 0
    cosines, sines = jnp.cos(phases_ref[...]), jnp.sin(phases_ref[...])
    for level in range(levels):
        merged = []
        for h in range(len(sources) // 2):
            stacked = []
            for child in range(2):
                stacked += turned(
                    sources[2 * h + child], cosines[row : row + 1], sines[row : row + 1]
                )
                row += 1
            product = jnp.dot(
                mats[level][h], jnp.concatenate(stacked, axis=0), preferred_element_type=jnp.float32
            )
            merged.append(product.astype(jnp.bfloat16))
        sources = merged
    total[...] += jnp.dot(sources[0], map_ref[0], preferred_element_type=jnp.float32)
    if final:
        width = rest[0].shape[1]
        strips = total.shape[1] // subs // width

        @pl.when(step == steps - 1)
        def _():
            for r in range(subs):
                for strip in range(strips):
                    start = pl.multiple_of((ids_ref[r] * strips + strip) * width, width)
                    out = rest[strip * subs + r]
                    out[...] = total[:, pl.ds(start, width)].astype(out.dtype)


def merge_blocks(sources, phases, mats, range_map, ids, before, final, first, length, unit):
    subs, levels = len(sources), len(mats)
    pieces, height = sources[0].shape[:2]
    columns = range_map.shape[2]
    beams = mats[-1].shape[1]
    steps = length * pieces
    given = before is not None

    def whole(array):
        return pl.BlockSpec(array.shape, lambda i, e, ids_ref: (0,) * array.ndim)

    in_specs = [pl.BlockSpec((1, height, unit), lambda i, e, ids_ref: (e, 0, i))] * subs
    local = range_map.shape[1]
    in_specs += [
        window(
            (phases.shape[0], unit), lambda i, e, ids_ref: (0, lanes(e * local + first + i * unit))
        )
    ]
    in_specs += [whole(mat) for mat in mats]
    in_specs += [
        window((1, unit, columns), lambda i, e, ids_ref: (e, lanes(first + i * unit), 0))
    ]
    operands = [ids, *sources, phases, *mats, range_map]
    scratch, aliases = [], {}
    if given:
        in_specs.append(pl.BlockSpec((beams, columns), lambda i, e, ids_ref: (0, 0)))
        operands.append(before)
    if final:
        strips = max(1, columns // subs // 128)
        width = columns // subs // strips
        out_shape = [jax.ShapeDtypeStruct((beams, width), jnp.bfloat16)] * (subs * strips)
        out_specs = [pl.BlockSpec((beams, width), lambda i, e, ids_ref: (0, 0))] * (subs * strips)
        scratch = [pltpu.VMEM((beams, columns), jnp.float32)]
    else:
        out_shape = jax.ShapeDtypeStruct((beams, columns), jnp.float32)
        out_specs = pl.BlockSpec((beams, columns), lambda i, e, ids_ref: (0, 0))
        if given:
            aliases = {len(operands) - 1: 0}
    flops = sum(2 * mat.size for mat in mats) * steps * unit + 2 * beams * columns * steps * unit
    moved = 2 * range_map.shape[2] * steps * unit + 2 * subs * height * steps * unit
    return pl.pallas_call(
        functools.partial(merge_kernel, levels, subs, given, final, steps),
        out_shape=out_shape,
        grid_spec=pltpu.PrefetchScalarGridSpec(
            num_scalar_prefetch=1,
            grid=(length, pieces),
            in_specs=in_specs,
            out_specs=out_specs,
            scratch_shapes=scratch,
        ),
        input_output_aliases=aliases,
        compiler_params=params(),
        cost_estimate=cost(flops, moved),
        name="merge_blocks",
    )(*operands)


def beam_kernel(subs, foot, ids_ref, *refs):
    pieces = refs[:subs]
    near_ref, far_ref, keep_ref, send_ref, held = refs[subs:]
    step = pl.program_id(0)
    count = pl.num_programs(0)

    @pl.when(step == 0)
    def _():
        total = pieces[0][...].astype(jnp.float32)
        for piece in pieces[1:]:
            total = total + piece[...].astype(jnp.float32)
        held[...] = total.astype(held.dtype)

    planes = keep_ref.shape[1]
    depth = held.shape[0] // planes
    for side, map_ref, out_ref in ((0, near_ref, keep_ref), (1, far_ref, send_ref)):
        tile = ids_ref[2 * step + side]
        covered = ids_ref[2 * count] == tile
        for entry in range(1, foot):
            covered = jnp.logical_or(covered, ids_ref[2 * count + entry] == tile)

        @pl.when(covered)
        def _():
            for plane in range(planes):
                out_ref[0, plane] = jnp.dot(
                    map_ref[0],
                    held[plane * depth : (plane + 1) * depth],
                    preferred_element_type=jnp.float32,
                ).astype(out_ref.dtype)

        @pl.when(jnp.logical_not(covered))
        def _():
            out_ref[...] = jnp.zeros_like(out_ref)


def beam_blocks(pieces, beam_map, ids):
    tiles, rows, depth = beam_map.shape
    count = tiles // 2
    height, width = pieces[0].shape
    planes = height // depth
    shape = (count, planes, rows, width)

    def pick(side):
        return pl.BlockSpec((1, rows, depth), lambda i, ids_ref: (ids_ref[2 * i + side], 0, 0))

    out_spec = pl.BlockSpec((1, planes, rows, width), lambda i, ids_ref: (i, 0, 0, 0))
    return pl.pallas_call(
        functools.partial(beam_kernel, len(pieces), ids.shape[0] - tiles),
        out_shape=[
            jax.ShapeDtypeStruct(shape, jnp.float32),
            jax.ShapeDtypeStruct(shape, jnp.bfloat16),
        ],
        grid_spec=pltpu.PrefetchScalarGridSpec(
            num_scalar_prefetch=1,
            grid=(count,),
            in_specs=[pl.BlockSpec((height, width), lambda i, ids_ref: (0, 0))] * len(pieces)
            + [pick(0), pick(1)],
            out_specs=[out_spec, out_spec],
            scratch_shapes=[pltpu.VMEM((height, width), jnp.bfloat16)],
        ),
        compiler_params=params(),
        cost_estimate=cost(2 * tiles * rows * depth * planes * width, 2 * beam_map.size),
        name="beam_blocks",
    )(ids, *pieces, beam_map, beam_map)


def own_first(pair, upper):
    return jnp.stack([jnp.where(upper == 1, pair[1 - c], pair[c]) for c in range(2)])


def angle_packets(angles, gates, base, piece):
    sub_index, subs = lax.axis_index("sub"), lax.axis_size("sub")
    levels = subs.bit_length() - 1
    packets = []
    for level in range(levels):
        beams = base << level
        higher = sub_index >> (level + 1)
        for h in range(subs >> (level + 1)):
            start = 2 * beams
            for bit in range(levels - level - 1):
                start = start + (((higher ^ h) >> bit) & 1) * (gates >> (level + 2 + bit))
            packet = jnp.concatenate(
                [
                    angles[level, :, : 2 * beams],
                    lax.dynamic_slice_in_dim(angles[level], start, piece, 1),
                ],
                axis=1,
            )
            packets.append(swap(packet, "sub", h << (level + 1)) if h else packet)
    return packets


def merge_tables(interp, packets, base):
    sub_index, subs = lax.axis_index("sub"), lax.axis_size("sub")
    levels = subs.bit_length() - 1
    mats, rows, offset = [], [], 0
    packets = list(packets)
    for level in range(levels):
        beams = base << level
        upper = (sub_index >> level) & 1
        size = 4 * beams * beams
        weights = interp[offset : offset + size].reshape(2, 2 * beams, beams).astype(jnp.float32)
        offset += size
        weights = own_first(weights, upper) * (2.0 * beams) ** -0.5
        group = []
        for _ in range(subs >> (level + 1)):
            packet = own_first(packets.pop(0), upper)
            cosine, sine = jnp.cos(packet[:, : 2 * beams]), jnp.sin(packet[:, : 2 * beams])
            real = cosine[:, :, None] * weights
            imag = sine[:, :, None] * weights
            group.append(
                jnp.concatenate(
                    [
                        jnp.concatenate([real[0], -imag[0], real[1], -imag[1]], axis=1),
                        jnp.concatenate([imag[0], real[0], imag[1], real[1]], axis=1),
                    ],
                    axis=0,
                ).astype(jnp.bfloat16)
            )
            rows.append(packet[:, 2 * beams :])
        mats.append(jnp.stack(group))
    missing = -2 * len(rows) % 8
    if missing:
        rows.append(jnp.zeros((missing, rows[0].shape[1]), jnp.float32))
    return mats, jnp.concatenate(rows)


def on_device(echoes, steering, interp, angles, range_map, beam_map, footprint):
    tiles, subs = lax.axis_size("tile"), lax.axis_size("sub")
    tile_index, sub_index = lax.axis_index("tile"), lax.axis_index("sub")
    pieces = tiles // subs
    local = echoes.shape[2]
    echoes = pltpu.with_memory_space_constraint(echoes, pltpu.HBM)
    base = steering.shape[1]
    unit = local // PARTS
    bits = subs.bit_length() - 1

    sources = [tile_index ^ k for k in range(tiles)]
    slots = [sub_index ^ mirrored(source // pieces, bits) for source in sources]
    spots = [source % pieces for source in sources]
    ids = jnp.stack(sources + slots + spots).astype(jnp.int32)
    column_ids = jnp.stack([sub_index ^ r for r in range(subs)]).astype(jnp.int32)

    stretches, first = [], 0
    for share in CHUNKS:
        stretches.append((first * unit, share * unit))
        first += share
    opening = stretches[0][1]

    cuts = cut_blocks(echoes, ids, 0, 1, opening, base)
    arrived = [[swap(cut, "tile", k) for cut, k in zip(cuts, masks(tiles))]]
    lent = lend_blocks(echoes, ids, opening, 1, local - opening, base)
    lent = swap(lent, "tile", 1)
    steer = jnp.concatenate(
        [
            jnp.concatenate([steering[0], -steering[1]], axis=1),
            jnp.concatenate([steering[1], steering[0]], axis=1),
        ],
        axis=0,
    )
    angles, cuts = lax.optimization_barrier((angles, cuts))
    packets = angle_packets(angles[0, 0], local * tiles, base, local * pieces)
    for part_id, (first, length) in list(enumerate(stretches))[1:]:
        joined = join_blocks(echoes, lent, ids, first, opening, 1, length, base)
        arrived.append([swap(part, "tile", 2 * d) for part, d in zip(joined, masks(tiles // 2))])
        if part_id == 1:
            interp, packets, _ = lax.optimization_barrier((interp, packets, joined[-1]))
            mats, phases = merge_tables(interp, packets, base)

    map_rows = range_map[0].reshape(pieces, local, range_map.shape[2])
    map_rows = pltpu.with_memory_space_constraint(map_rows, pltpu.HBM)

    totals = [None, None]
    for (first, length), blocks in zip(stretches, arrived):
        parts = steer_blocks(
            echoes,
            lent if first else None,
            blocks,
            steer,
            ids,
            first,
            opening,
            1,
            length,
            base,
            [] if totals[-2] is None else [totals[-2]],
        )
        parts = [parts[0]] + [swap(parts[r], "sub", r) for r in range(1, subs)]
        final = first + length == local
        merged = merge_blocks(
            parts,
            phases,
            mats,
            map_rows,
            column_ids,
            totals[-1],
            final,
            first,
            1,
            length,
        )
        totals.append(merged)
    total = totals[-1]

    beam_ids = jnp.concatenate([jnp.stack(sources).astype(jnp.int32), footprint[0]])
    strips = []
    for strip in range(len(total) // subs):
        mine = total[strip * subs : (strip + 1) * subs]
        strips.append([mine[0]] + [swap(mine[r], "sub", r) for r in range(1, subs)])
    images = []
    for quarters in strips:
        keep, send = beam_blocks(quarters, beam_map[0], beam_ids)
        other = swap(send, "tile", 1)
        image = keep[0] + other[0].astype(jnp.float32)
        for d in masks(tiles // 2):
            part = (keep[d] + other[d].astype(jnp.float32)).astype(jnp.bfloat16)
            part = swap(part, "tile", 2 * d)
            image = image + part.astype(jnp.float32)
        images.append(image)
    return jnp.concatenate(images, axis=2)


def solution(mesh):
    placed = (
        P(None, "sub", "tile"),
        P(None, ("sub", "tile"), None),
        P(),
        P("tile", "sub", None, None, None),
        P("tile", "sub", None),
        P("tile", None, None, None),
        P("tile", None),
    )

    return jax.shard_map(
        on_device, mesh=mesh, in_specs=placed, out_specs=P(None, "tile", "sub"), check_vma=False
    )
```

```python
import functools

import jax
import jax.numpy as jnp
from jax import lax
from jax.experimental import pallas as pl
from jax.experimental.pallas import tpu as pltpu
from jax.sharding import PartitionSpec as P


SHARES = (0, 7 / 16, 10 / 16, 13 / 16, 1)
GRANT = 24 << 20


def swap(block, axis, mask):
    count = lax.axis_size(axis)
    return lax.ppermute(block, axis, [(i, i ^ mask) for i in range(count)])


def cost(flops, nbytes):
    return pl.CostEstimate(flops=int(flops), bytes_accessed=int(nbytes), transcendentals=0)


def mirrored(value, bits):
    result = value * 0
    for low in range(bits):
        result = result | (((value >> low) & 1) << (bits - 1 - low))
    return result


def masks(count):
    return list(range(count - 1, 0, -1))


def lanes(start):
    return pl.multiple_of(start, 128)


def window(shape, offsets):
    return pl.BlockSpec(tuple(pl.Element(size) for size in shape), offsets)


def params():
    return pltpu.CompilerParams(vmem_limit_bytes=GRANT)


def block_of(rows, unit, first, pick):
    def offsets(i, ids_ref):
        return 0, pl.multiple_of(ids_ref[pick] * rows, rows), lanes(first + i * unit)

    return window((2, rows, unit), offsets)


def resident():
    return pl.BlockSpec(memory_space=pltpu.VMEM)


def fetch(echoes_ref, ids_ref, pick, first, out_ref, sem):
    rows, unit = out_ref.shape[1:]
    start = pl.multiple_of(ids_ref[pick] * rows, rows)
    source = echoes_ref.at[:, pl.ds(start, rows), pl.ds(first, unit)]
    return pltpu.make_async_copy(source, out_ref, sem)


def cut_kernel(chosen, first, ids_ref, echoes_ref, *refs):
    outs, sems = refs[:-1], refs[-1]
    copies = [
        fetch(echoes_ref, ids_ref, k, first, outs[place], sems.at[place])
        for place, k in enumerate(chosen)
    ]
    for copy in copies:
        copy.start()
    for copy in copies:
        copy.wait()


def cut_blocks(echoes, ids, chosen, first, unit, rows):
    return pl.pallas_call(
        functools.partial(cut_kernel, chosen, first),
        out_shape=[jax.ShapeDtypeStruct((2, rows, unit), echoes.dtype)] * len(chosen),
        grid_spec=pltpu.PrefetchScalarGridSpec(
            num_scalar_prefetch=1,
            grid=(1,),
            in_specs=[pl.BlockSpec(memory_space=pl.ANY)],
            out_specs=[resident()] * len(chosen),
            scratch_shapes=[pltpu.SemaphoreType.DMA((len(chosen),))],
        ),
        compiler_params=params(),
        cost_estimate=cost(0, 8 * len(chosen) * rows * unit),
        name="cut_blocks",
    )(ids, echoes)


def lend_kernel(count, first, ids_ref, echoes_ref, out_ref, sems):
    copies = [
        fetch(echoes_ref, ids_ref, 2 * d + 1, first, out_ref.at[d], sems.at[d])
        for d in range(count)
    ]
    for copy in copies:
        copy.start()
    for copy in copies:
        copy.wait()


def lend_blocks(echoes, ids, first, unit, rows):
    count = lax.axis_size("tile") // 2
    return pl.pallas_call(
        functools.partial(lend_kernel, count, first),
        out_shape=jax.ShapeDtypeStruct((count, 2, rows, unit), echoes.dtype),
        grid_spec=pltpu.PrefetchScalarGridSpec(
            num_scalar_prefetch=1,
            grid=(1,),
            in_specs=[pl.BlockSpec(memory_space=pl.ANY)],
            out_specs=resident(),
            scratch_shapes=[pltpu.SemaphoreType.DMA((count,))],
        ),
        compiler_params=params(),
        cost_estimate=cost(0, 8 * count * rows * unit),
        name="lend_blocks",
    )(ids, echoes)


def join_kernel(chosen, first, start, ids_ref, echoes_ref, lent_ref, *refs):
    outs, sems = refs[:-1], refs[-1]
    copies = [
        fetch(echoes_ref, ids_ref, 2 * d, first, outs[place].at[0], sems.at[place])
        for place, d in enumerate(chosen)
    ]
    for copy in copies:
        copy.start()
    for place, d in enumerate(chosen):
        outs[place][1] = lent_ref[d, :, :, start : start + outs[place].shape[3]]
    for copy in copies:
        copy.wait()


def join_blocks(echoes, lent, ids, first, behind, unit, rows):
    chosen = masks(lax.axis_size("tile") // 2)
    return pl.pallas_call(
        functools.partial(join_kernel, chosen, first, first - behind),
        out_shape=[jax.ShapeDtypeStruct((2, 2, rows, unit), echoes.dtype)] * len(chosen),
        grid_spec=pltpu.PrefetchScalarGridSpec(
            num_scalar_prefetch=1,
            grid=(1,),
            in_specs=[pl.BlockSpec(memory_space=pl.ANY), resident()],
            out_specs=[resident()] * len(chosen),
            scratch_shapes=[pltpu.SemaphoreType.DMA((len(chosen),))],
        ),
        compiler_params=params(),
        cost_estimate=cost(0, 16 * len(chosen) * rows * unit),
        name="join_blocks",
    )(ids, echoes, lent)


def steer_kernel(count, subs, start, ids_ref, weights_ref, own_ref, *refs):
    outs, held = refs[-1 - subs : -1], refs[-1]
    weights = weights_ref[...]
    unit = own_ref.shape[2]
    for k in range(count):
        if k == 0:
            block = own_ref[...]
        elif start is None:
            block = refs[count - 1 - k][...]
        elif k == 1:
            block = refs[0][0, :, :, start : start + unit]
        else:
            block = refs[count // 2 - k // 2][k % 2]
        block = block.reshape(block.shape[0] * block.shape[1], unit)
        beams = jnp.dot(weights, block, preferred_element_type=jnp.float32)
        held[ids_ref[count + k], ids_ref[2 * count + k]] = beams.astype(held.dtype)
    for r in range(subs):
        outs[r][...] = held[r]


def steer_blocks(echoes, lent, arrived, weights, ids, first, behind, unit, rows, after):
    count, subs = lax.axis_size("tile"), lax.axis_size("sub")
    pieces = count // subs
    height = weights.shape[0]
    operands = ([] if lent is None else [lent]) + arrived
    shape = (pieces, height, unit)
    return pl.pallas_call(
        functools.partial(steer_kernel, count, subs, None if lent is None else first - behind),
        out_shape=[jax.ShapeDtypeStruct(shape, echoes.dtype)] * subs,
        grid_spec=pltpu.PrefetchScalarGridSpec(
            num_scalar_prefetch=1,
            grid=(1,),
            in_specs=[resident(), block_of(rows, unit, first, 0)]
            + [resident()] * len(operands)
            + [pl.BlockSpec(memory_space=pl.ANY)] * len(after),
            out_specs=[resident()] * subs,
            scratch_shapes=[pltpu.VMEM((subs,) + shape, echoes.dtype)],
        ),
        compiler_params=params(),
        cost_estimate=cost(2 * count * height * height * unit, 4 * count * height * unit),
        name="steer_blocks",
    )(ids, weights, echoes, *operands, *after)


def turned(block, cosine, sine):
    half = block.shape[0] // 2
    real = block[:half].astype(jnp.float32)
    imag = block[half:].astype(jnp.float32)
    return jnp.concatenate(
        [
            (real * cosine - imag * sine).astype(jnp.bfloat16),
            (real * sine + imag * cosine).astype(jnp.bfloat16),
        ],
        axis=0,
    )


def merge_kernel(levels, subs, given, final, first, ids_ref, *refs):
    phases_ref = refs[subs]
    mats = refs[subs + 1 : subs + 1 + levels]
    map_ref = refs[subs + 1 + levels]
    rest = refs[subs + 2 + levels : -2]
    held, sems = refs[-2:]
    pieces, local = map_ref.shape[:2]
    unit = held.shape[0] // pieces
    copies = [
        pltpu.make_async_copy(
            map_ref.at[e, pl.ds(first, unit)], held.at[pl.ds(e * unit, unit)], sems.at[e]
        )
        for e in range(pieces)
    ]
    for copy in copies:
        copy.start()
    phases = jnp.concatenate(
        [phases_ref[:, e * local + first : e * local + first + unit] for e in range(pieces)], axis=1
    )
    cosines, sines = jnp.cos(phases), jnp.sin(phases)
    sources = [jnp.concatenate([ref[e] for e in range(pieces)], axis=1) for ref in refs[:subs]]
    row = 0
    for level in range(levels):
        merged = []
        for h in range(len(sources) // 2):
            children = [
                turned(
                    sources[2 * h + c],
                    cosines[row + c : row + c + 1],
                    sines[row + c : row + c + 1],
                )
                for c in range(2)
            ]
            row += 2
            product = jnp.dot(
                mats[level][h],
                jnp.concatenate(children, axis=0),
                preferred_element_type=jnp.float32,
            )
            merged.append(product.astype(jnp.bfloat16))
        sources = merged
    for copy in copies:
        copy.wait()
    if given:
        before, rest = rest[0], rest[1:]
    columns = held.shape[1]
    width = columns // subs
    for r in range(subs):
        start = r * width
        if final:
            start = pl.multiple_of(ids_ref[r] * width, width)
        part = pl.ds(start, width)
        share = jnp.dot(sources[0], held[:, part], preferred_element_type=jnp.float32)
        if given:
            share = before[:, part] + share
        if final:
            strips = len(rest) // subs
            for strip in range(strips):
                out = rest[strip * subs + r]
                span = out.shape[1]
                out[...] = share[:, strip * span : (strip + 1) * span].astype(out.dtype)
        else:
            rest[0][:, part] = share


def merge_blocks(sources, phases, mats, range_map, ids, before, final, first):
    subs, levels = len(sources), len(mats)
    pieces, height, unit = sources[0].shape
    columns = range_map.shape[2]
    beams = mats[-1].shape[1]
    given = before is not None
    operands = [*sources, phases, *mats]
    in_specs = [resident()] * len(operands) + [pl.BlockSpec(memory_space=pl.ANY)]
    operands = [ids, *operands, range_map]
    aliases = {}
    if given:
        in_specs.append(resident())
        operands.append(before)
    if final:
        strips = max(1, columns // subs // 128)
        width = columns // subs // strips
        out_shape = [jax.ShapeDtypeStruct((beams, width), jnp.bfloat16)] * (subs * strips)
        out_specs = [resident()] * (subs * strips)
    else:
        out_shape = jax.ShapeDtypeStruct((beams, columns), jnp.float32)
        out_specs = resident()
        if given:
            aliases = {len(operands) - 1: 0}
    gates = pieces * unit
    flops = sum(2 * mat.size for mat in mats) * gates + 2 * beams * columns * gates
    return pl.pallas_call(
        functools.partial(merge_kernel, levels, subs, given, final, first),
        out_shape=out_shape,
        grid_spec=pltpu.PrefetchScalarGridSpec(
            num_scalar_prefetch=1,
            grid=(1,),
            in_specs=in_specs,
            out_specs=out_specs,
            scratch_shapes=[
                pltpu.VMEM((gates, columns), range_map.dtype),
                pltpu.SemaphoreType.DMA((pieces,)),
            ],
        ),
        input_output_aliases=aliases,
        compiler_params=params(),
        cost_estimate=cost(flops, 2 * columns * gates + 2 * subs * height * gates),
        name="merge_blocks",
    )(*operands)


def beam_kernel(subs, foot, ids_ref, *refs):
    pieces = refs[:subs]
    near_ref, far_ref, keep_ref, send_ref, held = refs[subs:]
    step = pl.program_id(0)
    count = pl.num_programs(0)

    @pl.when(step == 0)
    def _():
        total = pieces[0][...].astype(jnp.float32)
        for piece in pieces[1:]:
            total = total + piece[...].astype(jnp.float32)
        held[...] = total.astype(held.dtype)

    planes = keep_ref.shape[1]
    depth = held.shape[0] // planes
    for side, map_ref, out_ref in ((0, near_ref, keep_ref), (1, far_ref, send_ref)):
        tile = ids_ref[2 * step + side]
        covered = ids_ref[2 * count] == tile
        for entry in range(1, foot):
            covered = jnp.logical_or(covered, ids_ref[2 * count + entry] == tile)

        @pl.when(covered)
        def _():
            for plane in range(planes):
                out_ref[step, plane] = jnp.dot(
                    map_ref[0],
                    held[plane * depth : (plane + 1) * depth],
                    preferred_element_type=jnp.float32,
                ).astype(out_ref.dtype)

        @pl.when(jnp.logical_not(covered))
        def _():
            out_ref[step] = jnp.zeros(out_ref.shape[1:], out_ref.dtype)


def beam_blocks(pieces, beam_map, ids):
    tiles, rows, depth = beam_map.shape
    count = tiles // 2
    height, width = pieces[0].shape
    planes = height // depth
    shape = (count, planes, rows, width)

    def pick(side):
        return pl.BlockSpec((1, rows, depth), lambda i, ids_ref: (ids_ref[2 * i + side], 0, 0))

    return pl.pallas_call(
        functools.partial(beam_kernel, len(pieces), ids.shape[0] - tiles),
        out_shape=[
            jax.ShapeDtypeStruct(shape, jnp.float32),
            jax.ShapeDtypeStruct(shape, jnp.bfloat16),
        ],
        grid_spec=pltpu.PrefetchScalarGridSpec(
            num_scalar_prefetch=1,
            grid=(count,),
            in_specs=[resident()] * len(pieces)
            + [pick(0), pick(1)],
            out_specs=[resident(), resident()],
            scratch_shapes=[pltpu.VMEM((height, width), jnp.bfloat16)],
        ),
        compiler_params=params(),
        cost_estimate=cost(2 * tiles * rows * depth * planes * width, 2 * beam_map.size),
        name="beam_blocks",
    )(ids, *pieces, beam_map, beam_map)


def own_first(pair, upper):
    return jnp.stack([jnp.where(upper == 1, pair[1 - c], pair[c]) for c in range(2)])


def angle_packets(angles, gates, base, piece):
    sub_index, subs = lax.axis_index("sub"), lax.axis_size("sub")
    levels = subs.bit_length() - 1
    packets = []
    for level in range(levels):
        beams = base << level
        higher = sub_index >> (level + 1)
        for h in range(subs >> (level + 1)):
            start = 2 * beams
            for bit in range(levels - level - 1):
                start = start + (((higher ^ h) >> bit) & 1) * (gates >> (level + 2 + bit))
            packet = jnp.concatenate(
                [
                    angles[level, :, : 2 * beams],
                    lax.dynamic_slice_in_dim(angles[level], start, piece, 1),
                ],
                axis=1,
            )
            packets.append(swap(packet, "sub", h << (level + 1)) if h else packet)
    return packets


def merge_tables(interp, packets, base):
    sub_index, subs = lax.axis_index("sub"), lax.axis_size("sub")
    levels = subs.bit_length() - 1
    mats, rows, offset = [], [], 0
    packets = list(packets)
    for level in range(levels):
        beams = base << level
        upper = (sub_index >> level) & 1
        size = 4 * beams * beams
        weights = interp[offset : offset + size].reshape(2, 2 * beams, beams).astype(jnp.float32)
        offset += size
        weights = own_first(weights, upper) * (2.0 * beams) ** -0.5
        group = []
        for _ in range(subs >> (level + 1)):
            packet = own_first(packets.pop(0), upper)
            cosine, sine = jnp.cos(packet[:, : 2 * beams]), jnp.sin(packet[:, : 2 * beams])
            real = cosine[:, :, None] * weights
            imag = sine[:, :, None] * weights
            group.append(
                jnp.concatenate(
                    [
                        jnp.concatenate([real[0], -imag[0], real[1], -imag[1]], axis=1),
                        jnp.concatenate([imag[0], real[0], imag[1], real[1]], axis=1),
                    ],
                    axis=0,
                ).astype(jnp.bfloat16)
            )
            rows.append(packet[:, 2 * beams :])
        mats.append(jnp.stack(group))
    missing = -2 * len(rows) % 8
    if missing:
        rows.append(jnp.zeros((missing, rows[0].shape[1]), jnp.float32))
    return mats, jnp.concatenate(rows)


def on_device(echoes, steering, interp, angles, range_map, beam_map, footprint):
    tiles, subs = lax.axis_size("tile"), lax.axis_size("sub")
    tile_index, sub_index = lax.axis_index("tile"), lax.axis_index("sub")
    pieces = tiles // subs
    local = echoes.shape[2]
    echoes = pltpu.with_memory_space_constraint(echoes, pltpu.HBM)
    base = steering.shape[1]
    bits = subs.bit_length() - 1

    sources = [tile_index ^ k for k in range(tiles)]
    slots = [sub_index ^ mirrored(source // pieces, bits) for source in sources]
    spots = [source % pieces for source in sources]
    ids = jnp.stack(sources + slots + spots).astype(jnp.int32)
    column_ids = jnp.stack([sub_index ^ r for r in range(subs)]).astype(jnp.int32)

    ends = [int(share * local) // 128 * 128 for share in SHARES]
    stretches = [(one, two - one) for one, two in zip(ends, ends[1:])]
    opening = stretches[0][1]

    cuts = []
    for chosen in (masks(tiles)[:2], masks(tiles)[2:]):
        cuts += cut_blocks(echoes, ids, chosen, 0, opening, base)
    arrived = [[swap(cut, "tile", k) for cut, k in zip(cuts, masks(tiles))]]
    lent = lend_blocks(echoes, ids, opening, local - opening, base)
    lent = swap(lent, "tile", 1)
    steer = jnp.concatenate(
        [
            jnp.concatenate([steering[0], -steering[1]], axis=1),
            jnp.concatenate([steering[1], steering[0]], axis=1),
        ],
        axis=0,
    )
    angles, cuts = lax.optimization_barrier((angles, cuts))
    packets = angle_packets(angles[0, 0], local * tiles, base, local * pieces)
    for part_id, (first, length) in list(enumerate(stretches))[1:]:
        joined = join_blocks(echoes, lent, ids, first, opening, length, base)
        arrived.append([swap(part, "tile", 2 * d) for part, d in zip(joined, masks(tiles // 2))])
        if part_id == 1:
            interp, packets, _ = lax.optimization_barrier((interp, packets, joined[-1]))
            mats, phases = merge_tables(interp, packets, base)

    map_rows = range_map[0].reshape(pieces, local, range_map.shape[2])
    map_rows = pltpu.with_memory_space_constraint(map_rows, pltpu.HBM)

    totals = [None, None]
    for (first, length), blocks in zip(stretches, arrived):
        parts = steer_blocks(
            echoes,
            lent if first else None,
            blocks,
            steer,
            ids,
            first,
            opening,
            length,
            base,
            [] if totals[-2] is None or first + length == local else [totals[-2]],
        )
        parts = [parts[0]] + [swap(parts[r], "sub", r) for r in range(1, subs)]
        final = first + length == local
        merged = merge_blocks(parts, phases, mats, map_rows, column_ids, totals[-1], final, first)
        totals.append(merged)
    total = totals[-1]

    beam_ids = jnp.concatenate([jnp.stack(sources).astype(jnp.int32), footprint[0]])
    strips = []
    for strip in range(len(total) // subs):
        mine = total[strip * subs : (strip + 1) * subs]
        strips.append([mine[0]] + [swap(mine[r], "sub", r) for r in range(1, subs)])
    images = []
    for quarters in strips:
        keep, send = beam_blocks(quarters, beam_map[0], beam_ids)
        other = swap(send, "tile", 1)
        image = keep[0] + other[0].astype(jnp.float32)
        for d in masks(tiles // 2):
            part = (keep[d] + other[d].astype(jnp.float32)).astype(jnp.bfloat16)
            part = swap(part, "tile", 2 * d)
            image = image + part.astype(jnp.float32)
        images.append(image)
    return jnp.concatenate(images, axis=2)


def solution(mesh):
    placed = (
        P(None, "sub", "tile"),
        P(None, ("sub", "tile"), None),
        P(),
        P("tile", "sub", None, None, None),
        P("tile", "sub", None),
        P("tile", None, None, None),
        P("tile", None),
    )

    return jax.shard_map(
        on_device, mesh=mesh, in_specs=placed, out_specs=P(None, "tile", "sub"), check_vma=False
    )
```

```python
import functools

import jax
import jax.numpy as jnp
from jax import lax
from jax.experimental import pallas as pl
from jax.experimental.pallas import tpu as pltpu
from jax.sharding import PartitionSpec as P


SHARES = (0, 7 / 16, 10 / 16, 13 / 16, 1)
GRANT = 24 << 20


def swap(block, axis, mask):
    count = lax.axis_size(axis)
    return lax.ppermute(block, axis, [(i, i ^ mask) for i in range(count)])


def cost(flops, nbytes):
    return pl.CostEstimate(flops=int(flops), bytes_accessed=int(nbytes), transcendentals=0)


def mirrored(value, bits):
    result = value * 0
    for low in range(bits):
        result = result | (((value >> low) & 1) << (bits - 1 - low))
    return result


def masks(count):
    return list(range(count - 1, 0, -1))


def params():
    return pltpu.CompilerParams(vmem_limit_bytes=GRANT)


def resident():
    return pl.BlockSpec(memory_space=pltpu.VMEM)


def fetch(echoes_ref, ids_ref, pick, first, out_ref, sem):
    rows, unit = out_ref.shape[1:]
    start = pl.multiple_of(ids_ref[pick] * rows, rows)
    source = echoes_ref.at[:, pl.ds(start, rows), pl.ds(first, unit)]
    return pltpu.make_async_copy(source, out_ref, sem)


def cut_kernel(chosen, first, ids_ref, echoes_ref, *refs):
    outs, sems = refs[:-1], refs[-1]
    copies = [
        fetch(echoes_ref, ids_ref, k, first, outs[place], sems.at[place])
        for place, k in enumerate(chosen)
    ]
    for copy in copies:
        copy.start()
    for copy in copies:
        copy.wait()


def cut_blocks(echoes, ids, chosen, first, unit, rows):
    return pl.pallas_call(
        functools.partial(cut_kernel, chosen, first),
        out_shape=[jax.ShapeDtypeStruct((2, rows, unit), echoes.dtype)] * len(chosen),
        grid_spec=pltpu.PrefetchScalarGridSpec(
            num_scalar_prefetch=1,
            grid=(1,),
            in_specs=[pl.BlockSpec(memory_space=pl.ANY)],
            out_specs=[resident()] * len(chosen),
            scratch_shapes=[pltpu.SemaphoreType.DMA((len(chosen),))],
        ),
        compiler_params=params(),
        cost_estimate=cost(0, 8 * len(chosen) * rows * unit),
        name="cut_blocks",
    )(ids, echoes)


def lend_kernel(count, first, ids_ref, echoes_ref, out_ref, sems):
    copies = [
        fetch(echoes_ref, ids_ref, 2 * d + 1, first, out_ref.at[d], sems.at[d])
        for d in range(count)
    ]
    for copy in copies:
        copy.start()
    for copy in copies:
        copy.wait()


def lend_blocks(echoes, ids, first, unit, rows):
    count = lax.axis_size("tile") // 2
    return pl.pallas_call(
        functools.partial(lend_kernel, count, first),
        out_shape=jax.ShapeDtypeStruct((count, 2, rows, unit), echoes.dtype),
        grid_spec=pltpu.PrefetchScalarGridSpec(
            num_scalar_prefetch=1,
            grid=(1,),
            in_specs=[pl.BlockSpec(memory_space=pl.ANY)],
            out_specs=resident(),
            scratch_shapes=[pltpu.SemaphoreType.DMA((count,))],
        ),
        compiler_params=params(),
        cost_estimate=cost(0, 8 * count * rows * unit),
        name="lend_blocks",
    )(ids, echoes)


def join_kernel(chosen, first, start, ids_ref, echoes_ref, lent_ref, *refs):
    outs, sems = refs[:-1], refs[-1]
    copies = [
        fetch(echoes_ref, ids_ref, 2 * d, first, outs[place].at[0], sems.at[place])
        for place, d in enumerate(chosen)
    ]
    for copy in copies:
        copy.start()
    own = fetch(echoes_ref, ids_ref, 0, first, outs[-1], sems.at[len(chosen)])
    own.start()
    copies.append(own)
    for place, d in enumerate(chosen):
        outs[place][1] = lent_ref[d, :, :, start : start + outs[place].shape[3]]
    for copy in copies:
        copy.wait()


def join_blocks(echoes, lent, ids, first, behind, unit, rows):
    chosen = masks(lax.axis_size("tile") // 2)
    return pl.pallas_call(
        functools.partial(join_kernel, chosen, first, first - behind),
        out_shape=[jax.ShapeDtypeStruct((2, 2, rows, unit), echoes.dtype)] * len(chosen)
        + [jax.ShapeDtypeStruct((2, rows, unit), echoes.dtype)],
        grid_spec=pltpu.PrefetchScalarGridSpec(
            num_scalar_prefetch=1,
            grid=(1,),
            in_specs=[pl.BlockSpec(memory_space=pl.ANY), resident()],
            out_specs=[resident()] * (len(chosen) + 1),
            scratch_shapes=[pltpu.SemaphoreType.DMA((len(chosen) + 1,))],
        ),
        compiler_params=params(),
        cost_estimate=cost(0, 16 * len(chosen) * rows * unit),
        name="join_blocks",
    )(ids, echoes, lent)


def steer_kernel(count, subs, start, ids_ref, weights_ref, own_ref, *refs):
    outs, held = refs[-1 - subs : -1], refs[-1]
    weights = weights_ref[...]
    unit = own_ref.shape[2]
    for k in range(count):
        if k == 0:
            block = own_ref[...]
        elif start is None:
            block = refs[count - 1 - k][...]
        elif k == 1:
            block = refs[0][0, :, :, start : start + unit]
        else:
            block = refs[count // 2 - k // 2][k % 2]
        block = block.reshape(block.shape[0] * block.shape[1], unit)
        beams = jnp.dot(weights, block, preferred_element_type=jnp.float32)
        held[ids_ref[count + k], ids_ref[2 * count + k]] = beams.astype(held.dtype)
    for r in range(subs):
        outs[r][...] = held[r]


def steer_blocks(own, lent, arrived, weights, ids, first, behind, after):
    count, subs = lax.axis_size("tile"), lax.axis_size("sub")
    pieces = count // subs
    height, unit = weights.shape[0], own.shape[2]
    operands = ([] if lent is None else [lent]) + arrived
    shape = (pieces, height, unit)
    return pl.pallas_call(
        functools.partial(steer_kernel, count, subs, None if lent is None else first - behind),
        out_shape=[jax.ShapeDtypeStruct(shape, own.dtype)] * subs,
        grid_spec=pltpu.PrefetchScalarGridSpec(
            num_scalar_prefetch=1,
            grid=(1,),
            in_specs=[resident()] * (2 + len(operands))
            + [pl.BlockSpec(memory_space=pl.ANY)] * len(after),
            out_specs=[resident()] * subs,
            scratch_shapes=[pltpu.VMEM((subs,) + shape, own.dtype)],
        ),
        compiler_params=params(),
        cost_estimate=cost(2 * count * height * height * unit, 4 * count * height * unit),
        name="steer_blocks",
    )(ids, weights, own, *operands, *after)


def turned(block, cosine, sine):
    half = block.shape[0] // 2
    real = block[:half].astype(jnp.float32)
    imag = block[half:].astype(jnp.float32)
    return jnp.concatenate(
        [
            (real * cosine - imag * sine).astype(jnp.bfloat16),
            (real * sine + imag * cosine).astype(jnp.bfloat16),
        ],
        axis=0,
    )


def merge_kernel(levels, subs, given, final, first, ids_ref, *refs):
    phases_ref = refs[subs]
    mats = refs[subs + 1 : subs + 1 + levels]
    map_ref = refs[subs + 1 + levels]
    rest = refs[subs + 2 + levels : -2]
    held, sems = refs[-2:]
    pieces, local = map_ref.shape[:2]
    unit = held.shape[0] // pieces
    copies = [
        pltpu.make_async_copy(
            map_ref.at[e, pl.ds(first, unit)], held.at[pl.ds(e * unit, unit)], sems.at[e]
        )
        for e in range(pieces)
    ]
    for copy in copies:
        copy.start()
    phases = jnp.concatenate(
        [phases_ref[:, e * local + first : e * local + first + unit] for e in range(pieces)], axis=1
    )
    cosines, sines = jnp.cos(phases), jnp.sin(phases)
    sources = [jnp.concatenate([ref[e] for e in range(pieces)], axis=1) for ref in refs[:subs]]
    row = 0
    for level in range(levels):
        merged = []
        for h in range(len(sources) // 2):
            children = [
                turned(
                    sources[2 * h + c],
                    cosines[row + c : row + c + 1],
                    sines[row + c : row + c + 1],
                )
                for c in range(2)
            ]
            row += 2
            product = jnp.dot(
                mats[level][h],
                jnp.concatenate(children, axis=0),
                preferred_element_type=jnp.float32,
            )
            merged.append(product.astype(jnp.bfloat16))
        sources = merged
    for copy in copies:
        copy.wait()
    if given:
        before, rest = rest[0], rest[1:]
    columns = held.shape[1]
    width = columns // subs
    for r in range(subs):
        start = r * width
        if final:
            start = pl.multiple_of(ids_ref[r] * width, width)
        part = pl.ds(start, width)
        share = jnp.dot(sources[0], held[:, part], preferred_element_type=jnp.float32)
        if given:
            share = before[:, part] + share
        if final:
            strips = len(rest) // subs
            for strip in range(strips):
                out = rest[strip * subs + r]
                span = out.shape[1]
                out[...] = share[:, strip * span : (strip + 1) * span].astype(out.dtype)
        else:
            rest[0][:, part] = share


def merge_blocks(sources, phases, mats, range_map, ids, before, final, first):
    subs, levels = len(sources), len(mats)
    pieces, height, unit = sources[0].shape
    columns = range_map.shape[2]
    beams = mats[-1].shape[1]
    given = before is not None
    operands = [*sources, phases, *mats]
    in_specs = [resident()] * len(operands) + [pl.BlockSpec(memory_space=pl.ANY)]
    operands = [ids, *operands, range_map]
    aliases = {}
    if given:
        in_specs.append(resident())
        operands.append(before)
    if final:
        strips = max(1, columns // subs // 128)
        width = columns // subs // strips
        out_shape = [jax.ShapeDtypeStruct((beams, width), jnp.bfloat16)] * (subs * strips)
        out_specs = [resident()] * (subs * strips)
    else:
        out_shape = jax.ShapeDtypeStruct((beams, columns), jnp.float32)
        out_specs = resident()
        if given:
            aliases = {len(operands) - 1: 0}
    gates = pieces * unit
    flops = sum(2 * mat.size for mat in mats) * gates + 2 * beams * columns * gates
    return pl.pallas_call(
        functools.partial(merge_kernel, levels, subs, given, final, first),
        out_shape=out_shape,
        grid_spec=pltpu.PrefetchScalarGridSpec(
            num_scalar_prefetch=1,
            grid=(1,),
            in_specs=in_specs,
            out_specs=out_specs,
            scratch_shapes=[
                pltpu.VMEM((gates, columns), range_map.dtype),
                pltpu.SemaphoreType.DMA((pieces,)),
            ],
        ),
        input_output_aliases=aliases,
        compiler_params=params(),
        cost_estimate=cost(flops, 2 * columns * gates + 2 * subs * height * gates),
        name="merge_blocks",
    )(*operands)


def beam_kernel(subs, foot, ids_ref, *refs):
    pieces = refs[:subs]
    map_ref, keep_ref, send_ref, held = refs[subs:]
    count, planes = keep_ref.shape[:2]
    depth = held.shape[0] // planes
    total = pieces[0][...].astype(jnp.float32)
    for piece in pieces[1:]:
        total = total + piece[...].astype(jnp.float32)
    held[...] = total.astype(held.dtype)

    @pl.loop(0, count)
    def _(step):
        for side, out_ref in ((1, send_ref), (0, keep_ref)):
            tile = ids_ref[2 * step + side]
            covered = ids_ref[2 * count] == tile
            for entry in range(1, foot):
                covered = jnp.logical_or(covered, ids_ref[2 * count + entry] == tile)

            @pl.when(covered)
            def _():
                for plane in range(planes):
                    out_ref[step, plane] = jnp.dot(
                        map_ref[tile],
                        held[plane * depth : (plane + 1) * depth],
                        preferred_element_type=jnp.float32,
                    ).astype(out_ref.dtype)

            @pl.when(jnp.logical_not(covered))
            def _():
                out_ref[step] = jnp.zeros(out_ref.shape[1:], out_ref.dtype)


def beam_blocks(pieces, beam_map, ids):
    tiles, rows, depth = beam_map.shape
    count = tiles // 2
    height, width = pieces[0].shape
    planes = height // depth
    shape = (count, planes, rows, width)

    return pl.pallas_call(
        functools.partial(beam_kernel, len(pieces), ids.shape[0] - tiles),
        out_shape=[
            jax.ShapeDtypeStruct(shape, jnp.float32),
            jax.ShapeDtypeStruct(shape, jnp.bfloat16),
        ],
        grid_spec=pltpu.PrefetchScalarGridSpec(
            num_scalar_prefetch=1,
            grid=(1,),
            in_specs=[resident()] * (len(pieces) + 1),
            out_specs=[resident(), resident()],
            scratch_shapes=[pltpu.VMEM((height, width), jnp.bfloat16)],
        ),
        compiler_params=params(),
        cost_estimate=cost(2 * tiles * rows * depth * planes * width, 2 * beam_map.size),
        name="beam_blocks",
    )(ids, *pieces, beam_map)


def own_first(pair, upper):
    return jnp.stack([jnp.where(upper == 1, pair[1 - c], pair[c]) for c in range(2)])


def angle_packets(angles, gates, base, piece):
    sub_index, subs = lax.axis_index("sub"), lax.axis_size("sub")
    levels = subs.bit_length() - 1
    packets = []
    for level in range(levels):
        beams = base << level
        higher = sub_index >> (level + 1)
        for h in range(subs >> (level + 1)):
            start = 2 * beams
            for bit in range(levels - level - 1):
                start = start + (((higher ^ h) >> bit) & 1) * (gates >> (level + 2 + bit))
            packet = jnp.concatenate(
                [
                    angles[level, :, : 2 * beams],
                    lax.dynamic_slice_in_dim(angles[level], start, piece, 1),
                ],
                axis=1,
            )
            packets.append(swap(packet, "sub", h << (level + 1)) if h else packet)
    return packets


def merge_tables(interp, packets, base):
    sub_index, subs = lax.axis_index("sub"), lax.axis_size("sub")
    levels = subs.bit_length() - 1
    mats, rows, offset = [], [], 0
    packets = list(packets)
    for level in range(levels):
        beams = base << level
        upper = (sub_index >> level) & 1
        size = 4 * beams * beams
        weights = interp[offset : offset + size].reshape(2, 2 * beams, beams).astype(jnp.float32)
        offset += size
        weights = own_first(weights, upper) * (2.0 * beams) ** -0.5
        group = []
        for _ in range(subs >> (level + 1)):
            packet = own_first(packets.pop(0), upper)
            cosine, sine = jnp.cos(packet[:, : 2 * beams]), jnp.sin(packet[:, : 2 * beams])
            real = cosine[:, :, None] * weights
            imag = sine[:, :, None] * weights
            group.append(
                jnp.concatenate(
                    [
                        jnp.concatenate([real[0], -imag[0], real[1], -imag[1]], axis=1),
                        jnp.concatenate([imag[0], real[0], imag[1], real[1]], axis=1),
                    ],
                    axis=0,
                ).astype(jnp.bfloat16)
            )
            rows.append(packet[:, 2 * beams :])
        mats.append(jnp.stack(group))
    missing = -2 * len(rows) % 8
    if missing:
        rows.append(jnp.zeros((missing, rows[0].shape[1]), jnp.float32))
    return mats, jnp.concatenate(rows)


def on_device(echoes, steering, interp, angles, range_map, beam_map, footprint):
    tiles, subs = lax.axis_size("tile"), lax.axis_size("sub")
    tile_index, sub_index = lax.axis_index("tile"), lax.axis_index("sub")
    pieces = tiles // subs
    local = echoes.shape[2]
    echoes = pltpu.with_memory_space_constraint(echoes, pltpu.HBM)
    base = steering.shape[1]
    bits = subs.bit_length() - 1

    sources = [tile_index ^ k for k in range(tiles)]
    slots = [sub_index ^ mirrored(source // pieces, bits) for source in sources]
    spots = [source % pieces for source in sources]
    ids = jnp.stack(sources + slots + spots).astype(jnp.int32)
    column_ids = jnp.stack([sub_index ^ r for r in range(subs)]).astype(jnp.int32)

    ends = [int(share * local) // 128 * 128 for share in SHARES]
    stretches = [(one, two - one) for one, two in zip(ends, ends[1:])]
    opening = stretches[0][1]

    cuts = []
    for chosen in (masks(tiles)[:2], masks(tiles)[2:] + [0]):
        cuts += cut_blocks(echoes, ids, chosen, 0, opening, base)
    owns = [cuts[-1]]
    arrived = [[swap(cut, "tile", k) for cut, k in zip(cuts, masks(tiles))]]
    lent = lend_blocks(echoes, ids, opening, local - opening, base)
    lent = swap(lent, "tile", 1)
    steer = jnp.concatenate(
        [
            jnp.concatenate([steering[0], -steering[1]], axis=1),
            jnp.concatenate([steering[1], steering[0]], axis=1),
        ],
        axis=0,
    )
    angles, cuts = lax.optimization_barrier((angles, cuts))
    packets = angle_packets(angles[0, 0], local * tiles, base, local * pieces)
    for part_id, (first, length) in list(enumerate(stretches))[1:]:
        joined = join_blocks(echoes, lent, ids, first, opening, length, base)
        owns.append(joined[-1])
        arrived.append([swap(part, "tile", 2 * d) for part, d in zip(joined, masks(tiles // 2))])
        if part_id == 1:
            interp, packets, _ = lax.optimization_barrier((interp, packets, joined[-1]))
            mats, phases = merge_tables(interp, packets, base)

    map_rows = range_map[0].reshape(pieces, local, range_map.shape[2])
    map_rows = pltpu.with_memory_space_constraint(map_rows, pltpu.HBM)

    totals = [None, None]
    for part_id, ((first, length), blocks) in enumerate(zip(stretches, arrived)):
        parts = steer_blocks(
            owns[part_id],
            lent if first else None,
            blocks,
            steer,
            ids,
            first,
            opening,
            [] if totals[-2] is None or first + length == local else [totals[-2]],
        )
        parts = [parts[0]] + [swap(parts[r], "sub", r) for r in range(1, subs)]
        final = first + length == local
        merged = merge_blocks(parts, phases, mats, map_rows, column_ids, totals[-1], final, first)
        totals.append(merged)
    total = totals[-1]

    beam_ids = jnp.concatenate([jnp.stack(sources).astype(jnp.int32), footprint[0]])
    strips = []
    for strip in range(len(total) // subs):
        mine = total[strip * subs : (strip + 1) * subs]
        strips.append([mine[0]] + [swap(mine[r], "sub", r) for r in range(1, subs)])
    images = []
    for quarters in strips:
        keep, send = beam_blocks(quarters, beam_map[0], beam_ids)
        other = swap(send, "tile", 1)
        image = keep[0] + other[0].astype(jnp.float32)
        for d in masks(tiles // 2):
            part = (keep[d] + other[d].astype(jnp.float32)).astype(jnp.bfloat16)
            part = swap(part, "tile", 2 * d)
            image = image + part.astype(jnp.float32)
        images.append(image)
    return jnp.concatenate(images, axis=2)


def solution(mesh):
    placed = (
        P(None, "sub", "tile"),
        P(None, ("sub", "tile"), None),
        P(),
        P("tile", "sub", None, None, None),
        P("tile", "sub", None),
        P("tile", None, None, None),
        P("tile", None),
    )

    return jax.shard_map(
        on_device, mesh=mesh, in_specs=placed, out_specs=P(None, "tile", "sub"), check_vma=False
    )
```
